256 devices in a mesh: col: 64 (over x, y, z_lo), slab: 4 (over z_hi, core).
Axes of the slice: x: 4, y: 4, z: 8 (z_hi: 2, z_lo: 4; z = z_hi * 4 + z_lo), core: 2. Of those that a mesh axis runs over, the one named last changes fastest.
Arguments:
- offsets: float32 [2, 128, 256, 128], P(None, 'col', 'slab'), may hold values from 0 to 1
- velocity: float32 [2, 128, 256, 128], P(None, 'col', 'slab'), may hold values from -8 to 8
- particle_mass: float32 [128, 256, 128], P('col', 'slab'), may hold values from 0.5 to 2
- pressure_start: float32 [128, 256, 128], P('col', 'slab'), may hold values from -4 to 4
- counts: int32 [128, 256], P('col', 'slab'), may hold values from 1 to 128
- leaving_slot: int32 [512, 4, 128], P('col', 'slab'), may hold values from 0 to 16383
- leaving_count: int32 [512, 4], P('col', 'slab'), may hold values from 1 to 128
- leaving_side: int32 [512, 4], P('col', 'slab'), may hold values from 0 to 1
Outputs:
- density_ratio: float32 [128, 256, 128], P('col', 'slab')
- pressure: float32 [128, 256, 128], P('col', 'slab')
- acceleration: float32 [2, 128, 256, 128], P(None, 'col', 'slab')
- velocity_new: float32 [2, 128, 256, 128], P(None, 'col', 'slab')
- offsets_new: float32 [2, 128, 256, 128], P(None, 'col', 'slab')
- arrived: float32 [2, 6, 512, 4, 128], P(None, None, 'col', 'slab')
The draws below stay inside these ranges and needn't reach their ends.
Inputs may be any that keep to these rules, and one draw needn't show every extreme that they name: `counts`: a cell's particles fill its slots 0 to count - 1. `leaving_slot`: a slot of the sending device's own block of cells. `leaving_count`: the block's slots 0 to count - 1 carry particles. `leaving_side`: 0 sends the block to the lower col index, 1 to the higher.
All inputs are finite; a program needn't handle non-finite values.
Results may differ from the reference program's by a relative error of at most 0.0001.
Values sent between devices are 32-bit elements; how exact they have to be, the bound alone decides.
A program may use at most 64 MiB of HBM per device.

```python
import math
import jax
import jax.numpy as jnp
from jax import lax

SLOTS = 128
CX = 2
CZ = 64
MIGB = 8
ITERS = 3
NXC = 128
NZC = 256
N_COL = 64
N_SLAB = 4


def set_ends(array, rng, low, top_value):
    longest = array.shape.index(max(array.shape))
    spots = []
    for shift in (0, 1):
        where = [jax.random.randint(jax.random.fold_in(rng, axis), (), 0, length) for axis, length in enumerate(array.shape)]
        where[longest] = (where[longest] + shift) % array.shape[longest]
        spots.append(tuple(where))
    return array.at[spots[0]].set(low).at[spots[1]].set(top_value)


def block_levels(rng, extent, cuts, least, high):
    gain, own = 1.0, jax.random.fold_in(rng, 6)
    for axis_at, parts in cuts:
        heights = jnp.exp(jax.random.uniform(jax.random.fold_in(own, axis_at), (parts,), jnp.float32, least / len(cuts), high / len(cuts)))
        gain = gain * jnp.repeat(heights, extent[axis_at] // parts).reshape([-1 if axis == axis_at else 1 for axis in range(len(extent))])
    return gain


def bell_draw(stream_key, shape, scale, reach, split=(), held_as=jnp.bfloat16):
    array = scale * jax.random.normal(stream_key, shape, jnp.float32)
    if split:
        array = array * block_levels(stream_key, shape, split, -0.22, 0.18)
    return jnp.clip(array, -reach, reach).astype(held_as)


def setup_inputs(seed: int = 0) -> dict:
    streams_of = jax.random.split(jax.random.key(seed), 9)
    return {
        "offsets": jnp.clip(1.0 * jax.random.uniform(streams_of[0], (2, NXC, NZC, SLOTS), jnp.float32) ** block_levels(streams_of[0], (2, NXC, NZC, SLOTS), ((1, 64), (2, 4)), -0.2, 0.2), 0.0, 1.0),
        "velocity": bell_draw(streams_of[1], (2, NXC, NZC, SLOTS), 2.0, 8.0, ((1, 64), (2, 4)), jnp.float32),
        "particle_mass": jnp.clip(jnp.exp(math.log(2.0) - 1.3862944 * jax.random.uniform(streams_of[2], (NXC, NZC, SLOTS), jnp.float32) ** block_levels(streams_of[2], (NXC, NZC, SLOTS), ((0, 64), (1, 4)), -0.2, 0.2)), 0.5, 2.0),
        "pressure_start": bell_draw(streams_of[3], (NXC, NZC, SLOTS), 1.0, 4.0, ((0, 64), (1, 4)), jnp.float32),
        "counts": set_ends(jax.random.randint(streams_of[4], (NXC, NZC), 1, SLOTS + 1), jax.random.fold_in(streams_of[4], 1), 1, SLOTS).astype(jnp.int32),
        "leaving_slot": set_ends(jax.random.randint(streams_of[5], (MIGB * N_COL, N_SLAB, SLOTS), 0, CX * CZ * SLOTS), jax.random.fold_in(streams_of[5], 1), 0, (CX * CZ * SLOTS) - 1).astype(jnp.int32),
        "leaving_count": set_ends(jax.random.randint(streams_of[6], (MIGB * N_COL, N_SLAB), 1, SLOTS + 1), jax.random.fold_in(streams_of[6], 1), 1, SLOTS).astype(jnp.int32),
        "leaving_side": set_ends(jax.random.randint(streams_of[7], (MIGB * N_COL, N_SLAB), 0, 2), jax.random.fold_in(streams_of[7], 1), 0, 1).astype(jnp.int32),
    }


TIME_STEP = 0.1
REST_DENSITY = 50.0
COMPRESSION = 2.0
RELAXATION = 0.5
GRAVITY = 1.0


def geometry(center, neighbor, shift_x, shift_z):
    delta_x = center[0][:, :, None] - neighbor[0][:, None, :] - shift_x
    delta_z = center[1][:, :, None] - neighbor[1][:, None, :] - shift_z
    support = jnp.maximum(1.0 - delta_x * delta_x - delta_z * delta_z, 0.0)
    return delta_x, delta_z, support


def density_terms(center, neighbor, shift_x, shift_z):
    delta_x, delta_z, support = geometry(center, neighbor, shift_x, shift_z)
    kernel = support * support * support
    slope = 6.0 * support * support
    masses = neighbor[4][:, None, :]
    approach = (center[2][:, :, None] - neighbor[2][:, None, :]) * delta_x + (center[3][:, :, None] - neighbor[3][:, None, :]) * delta_z
    return jnp.stack([jnp.sum(masses * kernel, -1), -jnp.sum(masses * slope * approach, -1)])


def jacobi_terms(center, neighbor, shift_x, shift_z):
    delta_x, delta_z, support = geometry(center, neighbor, shift_x, shift_z)
    slope = 6.0 * support * support
    return jnp.stack([jnp.sum(neighbor[2][:, None, :] * slope, -1), jnp.sum(neighbor[3][:, None, :] * slope, -1)])


def force_terms(center, neighbor, shift_x, shift_z):
    delta_x, delta_z, support = geometry(center, neighbor, shift_x, shift_z)
    slope = 6.0 * support * support
    lifted = neighbor[2][:, None, :] * (neighbor[3][:, None, :] - center[3][:, :, None]) * slope
    return jnp.stack([jnp.sum(lifted * delta_x, -1), jnp.sum(lifted * delta_z, -1)])


def column_pass(extended, column_index, depth_cells, pair_terms):
    column_block = lax.dynamic_slice_in_dim(extended, column_index, 3, 1)
    center = column_block[:, 1, 1:depth_cells + 1]
    totals = None
    for shift_x in (-1, 0, 1):
        for shift_z in (-1, 0, 1):
            neighbor = column_block[:, 1 + shift_x, 1 + shift_z:1 + shift_z + depth_cells]
            term = pair_terms(center, neighbor, float(shift_x), float(shift_z))
            totals = term if totals is None else totals + term
    return totals


def sweep(extended, columns, depth_cells, pair_terms):
    def one_column(column_index):
        return column_pass(extended, column_index, depth_cells, pair_terms)

    totals = lax.map(one_column, jnp.arange(columns, dtype=jnp.int32))
    return jnp.moveaxis(totals, 0, 1)


def pad_cells(fields):
    return jnp.pad(fields, ((0, 0), (1, 1), (1, 1), (0, 0)))


def reference(offsets, velocity, particle_mass, pressure_start, counts, leaving_slot, leaving_count, leaving_side):
    columns, depth_cells, slot_count = counts.shape[0], counts.shape[1], offsets.shape[-1]
    alive_mask = jnp.arange(slot_count, dtype=jnp.int32)[None, None, :] < counts[:, :, None]
    live_mass = jnp.where(alive_mask, particle_mass, 0.0)
    base_fields = jnp.concatenate([offsets, velocity, live_mass[None]], 0)
    totals = sweep(pad_cells(base_fields), columns, depth_cells, density_terms)
    density = jnp.where(alive_mask, totals[0], 0.0)
    diverge = totals[1]
    density_ratio = density / REST_DENSITY
    weight = jnp.where(alive_mask, live_mass / jnp.where(alive_mask, density, 1.0), 0.0)
    source = jnp.where(alive_mask, (density + TIME_STEP * diverge - REST_DENSITY) / REST_DENSITY, 0.0)
    pressure = jnp.where(alive_mask, pressure_start, 0.0)
    for sweep_index in range(ITERS):
        stacked = jnp.concatenate([offsets, weight[None], (weight * pressure)[None]], 0)
        totals = sweep(pad_cells(stacked), columns, depth_cells, jacobi_terms)
        diagonal = COMPRESSION + totals[0]
        updated = (1.0 - RELAXATION) * pressure + RELAXATION * (source + totals[1]) / diagonal
        pressure = jnp.where(alive_mask, updated, 0.0)
    stacked = jnp.concatenate([offsets, weight[None], pressure[None]], 0)
    acceleration = jnp.where(alive_mask[None], sweep(pad_cells(stacked), columns, depth_cells, force_terms), 0.0)
    pulled = jnp.stack([acceleration[0], acceleration[1] - GRAVITY])
    velocity_new = jnp.where(alive_mask[None], velocity + TIME_STEP * pulled, 0.0)
    offsets_new = jnp.where(alive_mask[None], offsets + TIME_STEP * velocity_new, 0.0)
    state = jnp.concatenate([offsets_new, velocity_new, pressure[None], live_mass[None]], 0)
    tiles = state.reshape(6, N_COL, CX, N_SLAB, CZ, SLOTS).transpose(1, 3, 0, 2, 4, 5).reshape(N_COL, N_SLAB, 6, CX * CZ * SLOTS)
    chosen = leaving_slot.reshape(N_COL, MIGB, N_SLAB, SLOTS).transpose(0, 2, 1, 3).reshape(N_COL, N_SLAB, 1, MIGB * SLOTS)
    chosen = jnp.broadcast_to(chosen, (N_COL, N_SLAB, 6, MIGB * SLOTS))
    blocks = jnp.take_along_axis(tiles, chosen, axis=3).reshape(N_COL, N_SLAB, 6, MIGB, SLOTS)
    block_count = leaving_count.reshape(N_COL, MIGB, N_SLAB).transpose(0, 2, 1)[:, :, None, :, None]
    block_side = leaving_side.reshape(N_COL, MIGB, N_SLAB).transpose(0, 2, 1)[:, :, None, :, None]
    filled = jnp.arange(SLOTS, dtype=jnp.int32)[None, None, None, None, :] < block_count
    upward = jnp.where(filled & (block_side == 1), blocks, 0.0)
    downward = jnp.where(filled & (block_side == 0), blocks, 0.0)
    from_lower = jnp.concatenate([jnp.zeros_like(upward[:1]), upward[:-1]], 0)
    from_higher = jnp.concatenate([downward[1:], jnp.zeros_like(downward[:1])], 0)
    arrived = jnp.stack([from_lower, from_higher]).transpose(0, 3, 1, 4, 2, 5).reshape(2, 6, N_COL * MIGB, N_SLAB, SLOTS)
    return density_ratio, pressure, acceleration, velocity_new, offsets_new, arrived
```

```python
import functools

import jax
import jax.numpy as jnp
from jax import lax
from jax.experimental import pallas as pl
from jax.experimental.pallas import tpu as pltpu
from jax.sharding import PartitionSpec as P

ITERS = 3
TIME_STEP = 0.1
REST_DENSITY = 50.0
COMPRESSION = 2.0
RELAXATION = 0.5
GRAVITY = 1.0

MESH = pl.DeviceIdType.MESH
F32 = jnp.float32

X, Z, VX, VZ, MASS, P0, WEIGHT, P1, P2, P3 = range(10)
FIRST = 8
CELLS = 64
SLOTS = 128
BLOCKS = 16

OWN_TILES = (
    ((1, 0, False, True), (1, 1, True, True), (2, -1, True, True), (2, 0, True, True), (2, 1, True, True)),
    ((2, 0, False, True), (2, 1, True, True)),
)
HALO_TILES = (
    ((1, 1, True, False), (1, 0, True, False), (1, -1, True, False)),
    ((2, 1, True, False), (2, 0, True, False), (2, -1, True, False)),
)
EXTRA = (
    (1, -1, ((1, 1, True, False), (2, 1, True, False))),
    (2, -1, ((2, 1, True, False),)),
    (1, CELLS, ((2, -1, True, False),)),
)
OWN0, OWN1, EXTRA0, HALO0, HALO1 = 0, 320, 448, 452, 650
TILES = 848
PAD = 2
FIELDS = 5


class Phase:
    def __init__(self, outs, a_fields, b_rows, shared, b_factors, a_factors):
        self.outs = outs
        self.a_fields = a_fields
        self.b_rows = b_rows
        self.shared = shared
        self.b_factors = b_factors
        self.a_factors = a_factors


def kernel(
    base,
    edges,
    leaving_slot,
    leaving_count,
    leaving_side,
    ratio_out,
    pressure_out,
    accel_out,
    velocity_out,
    offsets_out,
    arrived_out,
    rows,
    slopes,
    columns,
    kept,
    lane_columns,
    lane_sums,
    column_sums,
    row_sums,
    edge_send,
    edge_recv_base,
    edge_recv,
    block_send,
    block_recv,
    local_sem,
    send_sem,
    recv_sem,
    *,
    n_col,
    n_slab,
):
    col = lax.axis_index("col")
    slab = lax.axis_index("slab")
    around = ((-1, 0), (1, 0), (0, -1), (0, 1), (-1, -1), (-1, 1), (1, -1), (1, 1))

    def there(shift):
        ok = None
        for size, me, step in ((n_col, col, shift[0]), (n_slab, slab, shift[1])):
            if step:
                one = (me > 0) if step < 0 else (me < size - 1)
                ok = one if ok is None else jnp.logical_and(ok, one)
        return ok

    def device(shift):
        return (col + shift[0], slab + shift[1])

    local = pltpu.make_async_copy(base, rows.at[X : P0 + 1, 1:3, FIRST : FIRST + CELLS, :], local_sem.at[0])
    local.start()

    zeros = jnp.zeros((8, SLOTS), F32)
    for field in range(10):
        for column in range(4):
            if column in (0, 3):

                def clear(i, carry, field=field, column=column):
                    rows[field, column, pl.ds(pl.multiple_of(i * 8, 8), 8), :] = zeros
                    return carry

                lax.fori_loop(0, 10, clear, 0)
            else:
                rows[field, column, 0:8, :] = zeros
                rows[field, column, FIRST + CELLS : FIRST + CELLS + 8, :] = zeros
    edge_recv_base[...] = jnp.zeros_like(edge_recv_base)
    edge_recv[...] = jnp.zeros_like(edge_recv)
    block_recv[...] = jnp.zeros_like(block_recv)
    for place in range(4):
        for o in (0, 1):
            lane_sums[place, o] = jnp.zeros((BLOCKS, 8, SLOTS), F32)
    for o in (0, 1):
        for c in (0, 1):
            column_sums[o, c] = jnp.zeros((SLOTS, SLOTS), F32)
    for place in range(7):
        for column in range(4):
            columns[place, column] = jnp.zeros((SLOTS, SLOTS), F32)

    barrier = pltpu.get_barrier_semaphore()
    for shift in around:

        @pl.when(there(shift))
        def _(shift=shift):
            pl.semaphore_signal(barrier, inc=1, device_id=device(shift), device_id_type=MESH)

    peers = sum(jnp.where(there(shift), 1, 0).astype(jnp.int32) for shift in around)
    pl.semaphore_wait(barrier, peers)

    def copy_of(step, n):
        shift = around[n]
        back = around.index((-shift[0], -shift[1]))
        if n < 2:
            own, far = (1, 3) if n == 0 else (2, 0)
            if step == 0:
                src = base.at[:, own - 1]
                dst = rows.at[X : P0 + 1, far, FIRST : FIRST + CELLS, :]
            else:
                src = rows.at[P0 + step, own, FIRST : FIRST + CELLS, :]
                dst = rows.at[P0 + step, far, FIRST : FIRST + CELLS, :]
        else:
            side = 0 if shift[1] < 0 else 1
            if step == 0:
                src = edges.at[side]
                dst = edge_recv_base.at[back - 2]
            else:
                src = edge_send.at[step - 1, side]
                dst = edge_recv.at[step - 1, back - 2]
        return shift, pltpu.make_async_remote_copy(
            src_ref=src,
            dst_ref=dst,
            send_sem=send_sem.at[step, n],
            recv_sem=recv_sem.at[step, back],
            device_id=device(shift),
            device_id_type=MESH,
        )

    def send(step):
        if step > 0:
            for side, at in ((0, FIRST), (1, FIRST + CELLS - 1)):
                for c in (0, 1):
                    edge_send[step - 1, side, c : c + 1, :] = rows[P0 + step, 1 + c, at : at + 1, :]
        for n in (2, 3, 0, 1, 4, 5, 6, 7):
            shift, copy = copy_of(step, n)

            @pl.when(there(shift))
            def _(copy=copy):
                copy.start()

    def receive(step, which):
        for n in which:
            shift, _ = copy_of(step, n)
            back = around.index((-shift[0], -shift[1]))
            _, mirror = copy_of(step, back)

            @pl.when(there(shift))
            def _(mirror=mirror):
                mirror.wait_recv()

        for n in which:
            if n < 2:
                continue
            shift = around[n]
            at = FIRST - 1 if shift[1] < 0 else FIRST + CELLS
            take = {0: ((1, 0), (2, 1)), -1: ((0, 1),), 1: ((3, 0),)}[shift[0]]
            for mine, theirs in take:
                if step == 0:
                    for field in range(6):
                        at_row = field * 2 + theirs
                        rows[field, mine, at : at + 1, :] = edge_recv_base[n - 2, at_row : at_row + 1, :]
                else:
                    rows[P0 + step, mine, at : at + 1, :] = edge_recv[step - 1, n - 2, theirs : theirs + 1, :]

    def finish_sends(step):
        for n in range(8):
            shift, copy = copy_of(step, n)

            @pl.when(there(shift))
            def _(copy=copy):
                copy.wait_send()

    def own_rows(field):
        return jnp.concatenate([rows[field, c, FIRST : FIRST + CELLS, :] for c in (1, 2)], axis=0)

    def set_own(field, value):
        for c in (0, 1):
            rows[field, 1 + c, FIRST : FIRST + CELLS, :] = value[c * CELLS : (c + 1) * CELLS]

    def prepare(phase, column, k, place):
        lane = jnp.full((8, SLOTS), k + FIRST, jnp.int32)
        for b in range(BLOCKS):
            for i, field in enumerate(phase.a_fields):
                part = columns[field, column, b * 8 : b * 8 + 8, :]
                lane_columns[place, i, b] = jnp.take_along_axis(part, lane, axis=1)

    def compute(phase, column, k, tiles, tile0, place):
        outs = phase.outs
        b_rows, theirs = [], []
        for other, dk, _, _ in tiles:

            def row(field, other=other, dk=dk):
                return jnp.broadcast_to(rows[field, other, pl.ds(k + (FIRST + dk), 1), :], (8, SLOTS))

            b_rows.append(phase.b_rows(row, float(other - column), float(dk)))
            theirs.append([[None, None] for _ in range(outs)])
        for b in range(BLOCKS):
            a = [lane_columns[place, i, b] for i in range(len(phase.a_fields))]
            a_factors = phase.a_factors(a)
            mine = [None] * outs
            for i, (_, _, give, take) in enumerate(tiles):
                shared = phase.shared(a, b_rows[i], (tile0 + i, slice(b * 8, b * 8 + 8)))
                for o in range(outs):
                    if take:
                        term = shared[o] * phase.b_factors(b_rows[i])[o]
                        mine[o] = term if mine[o] is None else mine[o] + term
                    if give:
                        term = shared[o] * a_factors[o]
                        so_far = theirs[i][o][b % 2]
                        theirs[i][o][b % 2] = term if so_far is None else so_far + term
            for o in range(outs):
                if mine[o] is not None:
                    lane_sums[place, o, b] = mine[o]
        for i, (other, dk, give, _) in enumerate(tiles):
            if give:
                for o in range(outs):
                    at = (o, other - 1, k + (PAD + dk))
                    row_sums[at] = row_sums[at] + (theirs[i][o][0] + theirs[i][o][1])

    def collect(phase, column, k, place):
        here = lax.broadcasted_iota(jnp.int32, (8, SLOTS), 1) == k + FIRST
        for b in range(BLOCKS):
            for o in range(phase.outs):
                total = jnp.sum(lane_sums[place, o, b], axis=1, keepdims=True)
                at = (o, column - 1, slice(b * 8, b * 8 + 8), slice(None))
                column_sums[at] = jnp.where(here, total, column_sums[at])

    def run(phase, step, transpose):
        def clear(i, carry):
            for o in range(phase.outs):
                row_sums[o, 0, i] = zeros
                row_sums[o, 1, i] = zeros
            return carry

        lax.fori_loop(0, CELLS + 2 * PAD, clear, 0)
        transpose((1, 2))

        def prepare_own(k, parity):
            prepare(phase, 1, k, 2 * parity)
            prepare(phase, 2, k, 2 * parity + 1)

        def compute_own(k, parity):
            compute(phase, 1, k, OWN_TILES[0], OWN0 + 5 * k, 2 * parity)
            compute(phase, 2, k, OWN_TILES[1], OWN1 + 2 * k, 2 * parity + 1)

        def collect_own(k, parity):
            collect(phase, 1, k, 2 * parity)
            collect(phase, 2, k, 2 * parity + 1)

        def own(i, carry):
            for parity in (0, 1):
                k = 1 + 2 * i + parity
                prepare_own(k + 1, 1 - parity)
                collect_own(k - 1, 1 - parity)
                compute_own(k, parity)
            return carry

        prepare_own(1, 0)
        lax.fori_loop(0, (CELLS - 2) // 2, own, 0)
        collect_own(CELLS - 2, 1)

        receive(step, range(8))
        transpose((0, 1, 2, 3))

        def ends(i, carry):
            k = i * (CELLS - 1)
            prepare_own(k, 0)
            compute_own(k, 0)
            collect_own(k, 0)
            return carry

        lax.fori_loop(0, 2, ends, 0)
        for i, (column, k, _) in enumerate(EXTRA):
            prepare(phase, column, k, i)
        tile0 = EXTRA0
        for i, (column, k, tiles) in enumerate(EXTRA):
            compute(phase, column, k, tiles, tile0, i)
            tile0 += len(tiles)

        def prepare_halo(k, parity):
            prepare(phase, 0, k, 2 * parity)
            prepare(phase, 3, k, 2 * parity + 1)

        def halo(i, carry):
            for parity in (0, 1):
                k = 2 * i + parity - 1
                prepare_halo(k + 1, 1 - parity)
                compute(phase, 0, k, HALO_TILES[0], HALO0 + 3 * (k + 1), 2 * parity)
                compute(phase, 3, k, HALO_TILES[1], HALO1 + 3 * (k + 1), 2 * parity + 1)
            return carry

        prepare_halo(-1, 0)
        lax.fori_loop(0, (CELLS + 2) // 2, halo, 0)

    def sums(o):
        parts = []
        for c in (0, 1):
            by_row = jnp.sum(row_sums[o, c, PAD : PAD + CELLS], axis=1)
            parts.append(by_row + column_sums[o, c].T[FIRST : FIRST + CELLS])
        return jnp.concatenate(parts, axis=0)

    def transpose_of(pairs):
        def of(which):
            for column in which:
                for place, value in pairs:
                    columns[place, column, :, 0:80] = value(column).T

        return of

    def field(f):
        return lambda column: rows[f, column]

    def product(f):
        return lambda column: rows[WEIGHT, column] * rows[f, column]

    def geometry_rows(row, shift_x, shift_z):
        return row(X) + shift_x, row(Z) + shift_z

    def density_rows(row, shift_x, shift_z):
        return (*geometry_rows(row, shift_x, shift_z), row(VX), row(VZ), row(MASS))

    def density_shared(a, b, at):
        dx = a[0] - b[0]
        dz = a[1] - b[1]
        support = jnp.maximum(1.0 - (dx * dx + dz * dz), 0.0)
        square = support * support
        slopes[at] = square
        approach = (a[2] - b[2]) * dx + (a[3] - b[3]) * dz
        return square * support, square * approach

    def first_rows(row, shift_x, shift_z):
        weight = row(WEIGHT)
        return weight, weight * row(P0)

    def next_rows(pressure_field):
        def of(row, shift_x, shift_z):
            return (row(WEIGHT) * row(pressure_field),)

        return of

    def force_rows(row, shift_x, shift_z):
        return (*geometry_rows(row, shift_x, shift_z), row(WEIGHT), row(P3))

    def force_shared(a, b, at):
        lifted = slopes[at] * (b[3] - a[3])
        return lifted * (a[0] - b[0]), lifted * (a[1] - b[1])

    def repeat(part, times):
        return lambda values: (values[part],) * times

    CW, CQ, CP = 4, 5, 6

    send(0)
    local.wait()
    run(
        Phase(2, (0, 1, 2, 3, 4), density_rows, density_shared, repeat(4, 2), repeat(4, 2)),
        0,
        transpose_of([(f, field(f)) for f in (X, Z, VX, VZ, MASS)]),
    )
    live_mass = own_rows(MASS)
    alive = live_mass > 0.0
    density = jnp.where(alive, sums(0), 0.0)
    diverge = -6.0 * sums(1)
    ratio = density / REST_DENSITY
    for c in (0, 1):
        ratio_out[c] = ratio[c * CELLS : (c + 1) * CELLS]
    weight = jnp.where(alive, 6.0 * live_mass / jnp.where(alive, density, 1.0), 0.0)
    set_own(WEIGHT, weight)
    send(1)
    kept[0] = jnp.where(alive, (density + TIME_STEP * diverge - REST_DENSITY) / REST_DENSITY, 0.0)
    for sweep in range(ITERS):
        pressure_field = P0 if sweep == 0 else P0 + 1 + sweep
        if sweep == 0:
            phase = Phase(
                2,
                (CW, CQ),
                first_rows,
                lambda a, b, at: (slopes[at],) * 2,
                lambda b: b,
                lambda a: a,
            )
            moved = [(CW, field(WEIGHT)), (CQ, product(P0))]
        else:
            phase = Phase(
                1,
                (CQ,),
                next_rows(pressure_field),
                lambda a, b, at: (slopes[at],),
                lambda b: b,
                lambda a: a,
            )
            moved = [(CQ, product(pressure_field))]
        run(phase, 1 + sweep, transpose_of(moved))
        if sweep == 0:
            kept[1] = COMPRESSION + sums(0)
            pulled = sums(1)
        else:
            pulled = sums(0)
        updated = (1.0 - RELAXATION) * own_rows(pressure_field) + RELAXATION * (kept[0] + pulled) / kept[1]
        pressure = jnp.where(own_rows(MASS) > 0.0, updated, 0.0)
        set_own(P1 + sweep, pressure)
        send(2 + sweep)
    for c in (0, 1):
        pressure_out[c] = pressure[c * CELLS : (c + 1) * CELLS]
    run(
        Phase(2, (X, Z, CW, CP), force_rows, force_shared, repeat(2, 2), repeat(2, 2)),
        4,
        transpose_of([(CP, field(P3))]),
    )

    live_mass = own_rows(MASS)
    alive = live_mass > 0.0
    for o in (0, 1):
        accel = jnp.where(alive, sums(o), 0.0)
        pulled = accel - GRAVITY if o == 1 else accel
        velocity_new = jnp.where(alive, own_rows(VX + o) + TIME_STEP * pulled, 0.0)
        offsets_new = jnp.where(alive, own_rows(X + o) + TIME_STEP * velocity_new, 0.0)
        for c in (0, 1):
            part = slice(c * CELLS, (c + 1) * CELLS)
            accel_out[o, c] = accel[part]
            velocity_out[o, c] = velocity_new[part]
            offsets_out[o, c] = offsets_new[part]
        columns[o, 0] = offsets_new.T
        columns[2 + o, 0] = velocity_new.T
    columns[4, 0] = own_rows(P3).T
    columns[5, 0] = live_mass.T

    chosen = leaving_slot[...]
    cell = chosen // SLOTS
    slot = chosen - cell * SLOTS
    lanes = lax.broadcasted_iota(jnp.int32, (8, SLOTS), 1)
    filled = lanes < leaving_count[...]
    upward = filled & (leaving_side[...] == 1)
    downward = filled & (leaving_side[...] == 0)
    sublanes = lax.broadcasted_iota(jnp.int32, (SLOTS, SLOTS), 0)
    cell_is, slot_is = [], []
    for b in range(8):
        cell_is.append(jnp.where(sublanes == cell[b : b + 1], 1.0, 0.0).astype(jnp.bfloat16))
    for comp in range(6):
        value = columns[comp, 0]
        high = value.astype(jnp.bfloat16)
        rest = value - high.astype(F32)
        middle = rest.astype(jnp.bfloat16)
        low = (rest - middle.astype(F32)).astype(jnp.bfloat16)
        picked = []
        for b in range(8):
            by_slot = sum(
                jnp.dot(part, cell_is[b], preferred_element_type=F32) for part in (low, middle, high)
            )
            one = jnp.where(sublanes == slot[b : b + 1], by_slot, 0.0)
            picked.append(jnp.sum(one, axis=0, keepdims=True))
        block = jnp.concatenate(picked, axis=0)
        block_send[0, comp] = jnp.where(downward, block, 0.0)
        block_send[1, comp] = jnp.where(upward, block, 0.0)

    def block_copy(n):
        return around[n], pltpu.make_async_remote_copy(
            src_ref=block_send.at[n],
            dst_ref=block_recv.at[1 - n],
            send_sem=send_sem.at[5, n],
            recv_sem=recv_sem.at[5, 1 - n],
            device_id=device(around[n]),
            device_id_type=MESH,
        )

    for n in (0, 1):
        shift, copy = block_copy(n)

        @pl.when(there(shift))
        def _(copy=copy):
            copy.start()

    for step in range(5):
        finish_sends(step)
    for n in (0, 1):
        shift, copy = block_copy(n)
        _, mirror = block_copy(1 - n)

        @pl.when(there(shift))
        def _(copy=copy, mirror=mirror):
            mirror.wait_recv()
            copy.wait_send()

    arrived_out[...] = block_recv[...]


def per_device(
    n_col,
    n_slab,
    offsets,
    velocity,
    particle_mass,
    pressure_start,
    counts,
    leaving_slot,
    leaving_count,
    leaving_side,
):
    alive = jnp.arange(SLOTS, dtype=jnp.int32)[None, None, :] < counts[:, :, None]
    live_mass = jnp.where(alive, particle_mass, 0.0)
    pressure = jnp.where(alive, pressure_start, 0.0)
    base = jnp.concatenate([offsets, velocity, live_mass[None], pressure[None]], 0)
    edges = jnp.stack([base[:, :, 0].reshape(12, SLOTS), base[:, :, CELLS - 1].reshape(12, SLOTS)])
    edges = jnp.pad(edges, ((0, 0), (0, 4), (0, 0)))
    vmem = pl.BlockSpec(memory_space=pltpu.VMEM)
    anywhere = pl.BlockSpec(memory_space=pl.ANY)
    cells = (2, CELLS, SLOTS)
    shape = lambda *s: jax.ShapeDtypeStruct(s, F32)
    results = pl.pallas_call(
        functools.partial(kernel, n_col=n_col, n_slab=n_slab),
        out_shape=(shape(*cells), shape(*cells), shape(2, *cells), shape(2, *cells), shape(2, *cells), shape(2, 6, 8, SLOTS)),
        in_specs=[anywhere, anywhere, vmem, vmem, vmem],
        out_specs=[vmem] * 6,
        scratch_shapes=[
            pltpu.VMEM((10, 4, 80, SLOTS), F32),
            pltpu.VMEM((TILES, SLOTS, SLOTS), F32),
            pltpu.VMEM((7, 4, SLOTS, SLOTS), F32),
            pltpu.VMEM((2, SLOTS, SLOTS), F32),
            pltpu.VMEM((4, FIELDS, BLOCKS, 8, SLOTS), F32),
            pltpu.VMEM((4, 2, BLOCKS, 8, SLOTS), F32),
            pltpu.VMEM((2, 2, SLOTS, SLOTS), F32),
            pltpu.VMEM((2, 2, CELLS + 2 * PAD, 8, SLOTS), F32),
            pltpu.VMEM((4, 2, 8, SLOTS), F32),
            pltpu.VMEM((6, 16, SLOTS), F32),
            pltpu.VMEM((4, 6, 8, SLOTS), F32),
            pltpu.VMEM((2, 6, 8, SLOTS), F32),
            pltpu.VMEM((2, 6, 8, SLOTS), F32),
            pltpu.SemaphoreType.DMA((1,)),
            pltpu.SemaphoreType.DMA((6, 8)),
            pltpu.SemaphoreType.DMA((6, 8)),
        ],
        compiler_params=pltpu.CompilerParams(
            collective_id=0, has_side_effects=True, vmem_limit_bytes=67_000_000
        ),
    )(
        base,
        edges,
        leaving_slot.reshape(8, SLOTS),
        jnp.broadcast_to(leaving_count, (8, SLOTS)),
        jnp.broadcast_to(leaving_side, (8, SLOTS)),
    )
    return (*results[:5], results[5].reshape(2, 6, 8, 1, SLOTS))


def solution(mesh):
    return jax.shard_map(
        functools.partial(per_device, mesh.shape["col"], mesh.shape["slab"]),
        mesh=mesh,
        in_specs=(
            P(None, "col", "slab", None),
            P(None, "col", "slab", None),
            P("col", "slab", None),
            P("col", "slab", None),
            P("col", "slab"),
            P("col", "slab", None),
            P("col", "slab"),
            P("col", "slab"),
        ),
        out_specs=(
            P("col", "slab", None),
            P("col", "slab", None),
            P(None, "col", "slab", None),
            P(None, "col", "slab", None),
            P(None, "col", "slab", None),
            P(None, None, "col", "slab", None),
        ),
        check_vma=False,
    )
```

```python
import functools

import jax
import jax.numpy as jnp
import numpy as np
from jax import lax
from jax.experimental import pallas as pl
from jax.experimental.pallas import tpu as pltpu
from jax.sharding import PartitionSpec as P

ITERS = 3
TIME_STEP = 0.1
REST_DENSITY = 50.0
COMPRESSION = 2.0
RELAXATION = 0.5
GRAVITY = 1.0

MESH = pl.DeviceIdType.MESH
F32 = jnp.float32

X, Z, VX, VZ, MASS, P0, WEIGHT, P1, P2, P3 = range(10)
FIRST = 8
CELLS = 64
SLOTS = 128
BLOCKS = 16

OWN_TILES = (
    ((1, 0, False, True), (1, 1, True, True), (2, -1, True, True), (2, 0, True, True), (2, 1, True, True)),
    ((2, 0, False, True), (2, 1, True, True)),
)
HALO_TILES = (
    ((1, 1, True, False), (1, 0, True, False), (1, -1, True, False)),
    ((2, 1, True, False), (2, 0, True, False), (2, -1, True, False)),
)
EXTRA = (
    (1, -1, ((1, 1, True, False), (2, 1, True, False))),
    (2, -1, ((2, 1, True, False),)),
    (1, CELLS, ((2, -1, True, False),)),
)
OWN0, OWN1, HALO0, HALO1 = 0, 320, 448, 646
TILES = 844
EXTRA_AT = (HALO0 + 1, HALO1 + 1, HALO1 + 2)
PAD = 2
FIELDS = 2
PARTS = 24

ONE = 21
SIX = ((0, 0), (0, 1), (1, 0), (1, 1), (0, 2), (2, 0))
FOUR = ((0, 0), (0, 1), (1, 0), (1, 1))
HALF = 32


def density_pairs(sx, sz):
    x, z, vx, vz, u, e = 0, 3, 6, 9, 12, 15
    near = [(ONE, ONE, 1 - sx * sx - sz * sz)]
    approach = []
    for a in range(3):
        near += [(u + a, ONE, 1), (ONE, u + a, 1)]
        approach += [(e + a, ONE, 1), (ONE, e + a, 1)]
    for f, v, s in ((x, vx, sx), (z, vz, sz)):
        near += [(f + a, f + b, 2) for a, b in SIX]
        approach += [(v + a, f + b, -1) for a, b in FOUR] + [(f + a, v + b, -1) for a, b in FOUR]
        for a in range(3):
            near += [(f + a, ONE, 2 * s), (ONE, f + a, -2 * s)]
        for a in range(2):
            approach += [(v + a, ONE, -s), (ONE, v + a, s)]
    return near, approach


def force_pairs(sx, sz):
    halves = []
    for f, g, s in ((0, 9, sx), (3, 12, sz)):
        half = [(f + a, 6 + b, 1) for a, b in SIX] + [(6 + a, f + b, 1) for a, b in SIX]
        for a in range(3):
            half += [(ONE, g + a, -1), (g + a, ONE, -1), (ONE, 6 + a, -s), (6 + a, ONE, s)]
        halves.append(half)
    return halves


def form_matrices():
    mine = np.zeros((2, PARTS, 2 * SLOTS), np.float32)
    others = np.zeros((2, 9, 2 * HALF, PARTS), np.float32)
    for form, (pairs, spread) in enumerate(((density_pairs, 18), (force_pairs, 15))):
        mine[form, spread : spread + 3, SLOTS:] = 1.0
        for sx in (-1, 0, 1):
            for sz in (-1, 0, 1):
                for half, terms in enumerate(pairs(sx, sz)):
                    for i, (a, b, factor) in enumerate(terms):
                        at = i + half * HALF
                        mine[form, a, at] = 1.0
                        others[form, (sx + 1) * 3 + sz + 1, at, b] = factor
    return jnp.asarray(mine, jnp.bfloat16), jnp.asarray(others, jnp.bfloat16)


class Phase:
    def __init__(self, outs, a_fields, b_rows, shared, b_factors=None, a_factors=None, form=None):
        self.outs = outs
        self.form = form
        self.a_fields = a_fields
        self.b_rows = b_rows
        self.shared = shared
        self.b_factors = b_factors
        self.a_factors = a_factors


def kernel(
    base,
    edges,
    leaving_slot,
    leaving_count,
    leaving_side,
    mine_matrix,
    others_matrix,
    ratio_out,
    pressure_out,
    accel_out,
    velocity_out,
    offsets_out,
    arrived_out,
    rows,
    slopes,
    cell_parts,
    selectors,
    kept,
    lane_columns,
    lane_terms,
    tile_terms,
    lane_sums,
    column_sums,
    row_sums,
    edge_send,
    edge_recv_base,
    edge_recv,
    block_send,
    block_recv,
    local_sem,
    send_sem,
    recv_sem,
    *,
    n_col,
    n_slab,
):
    col = lax.axis_index("col")
    slab = lax.axis_index("slab")
    around = ((-1, 0), (1, 0), (0, -1), (0, 1), (-1, -1), (-1, 1), (1, -1), (1, 1))

    def there(shift):
        ok = None
        for size, me, step in ((n_col, col, shift[0]), (n_slab, slab, shift[1])):
            if step:
                one = (me > 0) if step < 0 else (me < size - 1)
                ok = one if ok is None else jnp.logical_and(ok, one)
        return ok

    def device(shift):
        return (col + shift[0], slab + shift[1])

    local = pltpu.make_async_copy(base, rows.at[X : P0 + 1, 1:3, FIRST : FIRST + CELLS, :], local_sem.at[0])
    local.start()

    zeros = jnp.zeros((8, SLOTS), F32)
    for field in range(10):
        for column in range(4):
            if column in (0, 3):

                def clear(i, carry, field=field, column=column):
                    rows[field, column, pl.ds(pl.multiple_of(i * 8, 8), 8), :] = zeros
                    return carry

                lax.fori_loop(0, 10, clear, 0)
            else:
                rows[field, column, 0:8, :] = zeros
                rows[field, column, FIRST + CELLS : FIRST + CELLS + 8, :] = zeros
    edge_recv_base[...] = jnp.zeros_like(edge_recv_base)
    edge_recv[...] = jnp.zeros_like(edge_recv)
    block_recv[...] = jnp.zeros_like(block_recv)
    for place in range(4):
        for o in (0, 1):
            lane_sums[place, o] = jnp.zeros((BLOCKS, 8, SLOTS), F32)
    for o in (0, 1):
        for c in (0, 1):
            column_sums[o, c] = jnp.zeros((SLOTS, SLOTS), F32)

    def clear_parts(i, carry):
        for column in range(4):
            cell_parts[column, pl.ds(pl.multiple_of(i * 8, 8), 8), :] = zeros
        return carry

    lax.fori_loop(0, 80 * PARTS // 8, clear_parts, 0)
    part_of = lax.broadcasted_iota(jnp.int32, (PARTS, SLOTS), 0)
    for i in range(FIELDS):
        mine = (part_of >= 3 * i) & (part_of < 3 * i + 3)
        selectors[:, i * SLOTS : (i + 1) * SLOTS] = jnp.where(mine, 1.0, 0.0).astype(jnp.bfloat16)

    barrier = pltpu.get_barrier_semaphore()
    for shift in around:

        @pl.when(there(shift))
        def _(shift=shift):
            pl.semaphore_signal(barrier, inc=1, device_id=device(shift), device_id_type=MESH)

    peers = sum(jnp.where(there(shift), 1, 0).astype(jnp.int32) for shift in around)
    pl.semaphore_wait(barrier, peers)

    def copy_of(step, n):
        shift = around[n]
        back = around.index((-shift[0], -shift[1]))
        if n < 2:
            own, far = (1, 3) if n == 0 else (2, 0)
            if step == 0:
                src = base.at[:, own - 1]
                dst = rows.at[X : P0 + 1, far, FIRST : FIRST + CELLS, :]
            else:
                src = rows.at[P0 + step, own, FIRST : FIRST + CELLS, :]
                dst = rows.at[P0 + step, far, FIRST : FIRST + CELLS, :]
        else:
            side = 0 if shift[1] < 0 else 1
            if step == 0:
                src = edges.at[side]
                dst = edge_recv_base.at[back - 2]
            else:
                src = edge_send.at[step - 1, side]
                dst = edge_recv.at[step - 1, back - 2]
        return shift, pltpu.make_async_remote_copy(
            src_ref=src,
            dst_ref=dst,
            send_sem=send_sem.at[step, n],
            recv_sem=recv_sem.at[step, back],
            device_id=device(shift),
            device_id_type=MESH,
        )

    def send(step):
        if step > 0:
            for side, at in ((0, FIRST), (1, FIRST + CELLS - 1)):
                for c in (0, 1):
                    edge_send[step - 1, side, c : c + 1, :] = rows[P0 + step, 1 + c, at : at + 1, :]
        for n in (2, 3, 0, 1, 4, 5, 6, 7):
            shift, copy = copy_of(step, n)

            @pl.when(there(shift))
            def _(copy=copy):
                copy.start()

    def receive(step, which):
        for n in which:
            shift, _ = copy_of(step, n)
            back = around.index((-shift[0], -shift[1]))
            _, mirror = copy_of(step, back)

            @pl.when(there(shift))
            def _(mirror=mirror):
                mirror.wait_recv()

        for n in which:
            if n < 2:
                continue
            shift = around[n]
            at = FIRST - 1 if shift[1] < 0 else FIRST + CELLS
            take = {0: ((1, 0), (2, 1)), -1: ((0, 1),), 1: ((3, 0),)}[shift[0]]
            for mine, theirs in take:
                if step == 0:
                    for field in range(6):
                        at_row = field * 2 + theirs
                        rows[field, mine, at : at + 1, :] = edge_recv_base[n - 2, at_row : at_row + 1, :]
                else:
                    rows[P0 + step, mine, at : at + 1, :] = edge_recv[step - 1, n - 2, theirs : theirs + 1, :]

    def finish_sends(step):
        for n in range(8):
            shift, copy = copy_of(step, n)

            @pl.when(there(shift))
            def _(copy=copy):
                copy.wait_send()

    def own_rows(field):
        return jnp.concatenate([rows[field, c, FIRST : FIRST + CELLS, :] for c in (1, 2)], axis=0)

    def set_own(field, value):
        for c in (0, 1):
            rows[field, 1 + c, FIRST : FIRST + CELLS, :] = value[c * CELLS : (c + 1) * CELLS]

    def prepare(phase, column, k, place, tiles):
        fields = len(phase.a_fields)
        at = pl.multiple_of((k + FIRST) * PARTS, PARTS)
        parts = cell_parts[column, pl.ds(at, PARTS), :].astype(jnp.bfloat16)
        if phase.form is not None:
            spread = lax.dot_general(
                parts, mine_matrix[phase.form], (((0,), (0,)), ((), ())), preferred_element_type=F32
            )
            lane_terms[place] = spread[:, :SLOTS].astype(jnp.bfloat16)
            for i, (other, dk, _, _) in enumerate(tiles):
                at = pl.multiple_of((k + (FIRST + dk)) * PARTS, PARTS)
                parts = cell_parts[other, pl.ds(at, PARTS), :].astype(jnp.bfloat16)
                matrix = others_matrix[phase.form, (other - column + 1) * 3 + dk + 1]
                tile_terms[place, i] = jnp.dot(matrix, parts, preferred_element_type=F32).astype(jnp.bfloat16)
            for b in range(BLOCKS):
                lane_columns[place, 0, b] = spread[b * 8 : b * 8 + 8, SLOTS:]
            return
        spread = lax.dot_general(parts, selectors[:, 0 : fields * SLOTS], (((0,), (0,)), ((), ())), preferred_element_type=F32)
        for i in range(fields):
            for b in range(BLOCKS):
                lane_columns[place, i, b] = spread[b * 8 : b * 8 + 8, i * SLOTS : (i + 1) * SLOTS]

    def compute_form(phase, column, k, tiles, tile0, place):
        outs = phase.outs
        terms = lane_terms[place, :, : 2 * HALF]
        blank = jnp.zeros((HALF, SLOTS), jnp.bfloat16)

        def product_of(i):
            left = jnp.concatenate([tile_terms[place, i, :HALF], blank], axis=0)
            right = jnp.concatenate([blank, tile_terms[place, i, HALF:]], axis=0)
            return jnp.dot(terms, jnp.concatenate([left, right], axis=1), preferred_element_type=F32)

        following = product_of(0)
        for i, (other, dk, give, take) in enumerate(tiles):
            product = following
            if i + 1 < len(tiles):
                following = product_of(i + 1)
            if take:
                b_factor = jnp.broadcast_to(
                    rows[phase.b_rows, other, pl.ds(k + (FIRST + dk), 1), :], (8, SLOTS)
                )
            given = [[None, None] for _ in range(outs)]
            for b in range(BLOCKS):
                block = slice(b * 8, b * 8 + 8)
                shared = phase.shared(product[block, :SLOTS], product[block, SLOTS:], (tile0 + i, block))
                for o in range(outs):
                    if take:
                        term = shared[o] * b_factor
                        lane_sums[place, o, b] = term if i == 0 else lane_sums[place, o, b] + term
                    if give:
                        term = shared[o] * lane_columns[place, 0, b]
                        so_far = given[o][b % 2]
                        given[o][b % 2] = term if so_far is None else so_far + term
            if give:
                for o in range(outs):
                    at = (o, other - 1, k + (PAD + dk))
                    row_sums[at] = row_sums[at] + (given[o][0] + given[o][1])

    def compute(phase, column, k, tiles, tile0, place):
        if phase.form is not None:
            compute_form(phase, column, k, tiles, tile0, place)
            return
        outs = phase.outs
        b_rows, theirs = [], []
        for other, dk, _, _ in tiles:

            def row(field, other=other, dk=dk):
                return jnp.broadcast_to(rows[field, other, pl.ds(k + (FIRST + dk), 1), :], (8, SLOTS))

            b_rows.append(phase.b_rows(row, float(other - column), float(dk)))
            theirs.append([[None, None] for _ in range(outs)])
        for b in range(BLOCKS):
            a = [lane_columns[place, i, b] for i in range(len(phase.a_fields))]
            a_factors = phase.a_factors(a)
            mine = [None] * outs
            for i, (_, _, give, take) in enumerate(tiles):
                shared = phase.shared(a, b_rows[i], (tile0 + i, slice(b * 8, b * 8 + 8)))
                for o in range(outs):
                    if take:
                        term = shared[o] * phase.b_factors(b_rows[i])[o]
                        mine[o] = term if mine[o] is None else mine[o] + term
                    if give:
                        term = shared[o] * a_factors[o]
                        so_far = theirs[i][o][b % 2]
                        theirs[i][o][b % 2] = term if so_far is None else so_far + term
            for o in range(outs):
                if mine[o] is not None:
                    lane_sums[place, o, b] = mine[o]
        for i, (other, dk, give, _) in enumerate(tiles):
            if give:
                for o in range(outs):
                    at = (o, other - 1, k + (PAD + dk))
                    row_sums[at] = row_sums[at] + (theirs[i][o][0] + theirs[i][o][1])

    def collect(phase, column, k, place):
        here = lax.broadcasted_iota(jnp.int32, (8, SLOTS), 1) == k + FIRST
        for b in range(BLOCKS):
            for o in range(phase.outs):
                total = jnp.sum(lane_sums[place, o, b], axis=1, keepdims=True)
                at = (o, column - 1, slice(b * 8, b * 8 + 8), slice(None))
                column_sums[at] = jnp.where(here, total, column_sums[at])

    def run(phase, step, transpose):
        def clear(i, carry):
            for o in range(phase.outs):
                row_sums[o, 0, i] = zeros
                row_sums[o, 1, i] = zeros
            return carry

        lax.fori_loop(0, CELLS + 2 * PAD, clear, 0)
        transpose((1, 2))

        def prepare_own(k, parity):
            prepare(phase, 1, k, 2 * parity, OWN_TILES[0])
            prepare(phase, 2, k, 2 * parity + 1, OWN_TILES[1])

        def compute_own(k, parity):
            compute(phase, 1, k, OWN_TILES[0], OWN0 + 5 * k, 2 * parity)
            compute(phase, 2, k, OWN_TILES[1], OWN1 + 2 * k, 2 * parity + 1)

        def collect_own(k, parity):
            collect(phase, 1, k, 2 * parity)
            collect(phase, 2, k, 2 * parity + 1)

        def own(i, carry):
            for parity in (0, 1):
                k = 1 + 2 * i + parity
                collect_own(k - 2, parity)
                compute_own(k, parity)
                prepare_own(k + 2, parity)
            return carry

        prepare_own(1, 0)
        prepare_own(2, 1)
        lax.fori_loop(0, (CELLS - 2) // 2, own, 0)
        collect_own(CELLS - 3, 0)
        collect_own(CELLS - 2, 1)

        receive(step, range(8))
        transpose((0, 1, 2, 3))

        def ends(i, carry):
            k = i * (CELLS - 1)
            prepare_own(k, 0)
            compute_own(k, 0)
            collect_own(k, 0)
            return carry

        lax.fori_loop(0, 2, ends, 0)
        def prepare_halo(k, parity):
            prepare(phase, 0, k, 2 * parity, HALO_TILES[0])
            prepare(phase, 3, k, 2 * parity + 1, HALO_TILES[1])

        def halo(i, carry):
            for parity in (0, 1):
                k = 2 * i + parity - 1
                compute(phase, 0, k, HALO_TILES[0], HALO0 + 3 * (k + 1), 2 * parity)
                compute(phase, 3, k, HALO_TILES[1], HALO1 + 3 * (k + 1), 2 * parity + 1)
                prepare_halo(k + 2, parity)
            return carry

        prepare_halo(-1, 0)
        prepare_halo(0, 1)
        lax.fori_loop(0, (CELLS + 2) // 2, halo, 0)
        for i, (column, k, tiles) in enumerate(EXTRA):
            prepare(phase, column, k, i, tiles)
        for i, (column, k, tiles) in enumerate(EXTRA):
            compute(phase, column, k, tiles, EXTRA_AT[i], i)

    def sums(o):
        parts = []
        for c in (0, 1):
            by_row = jnp.sum(row_sums[o, c, PAD : PAD + CELLS], axis=1)
            parts.append(by_row + column_sums[o, c].T[FIRST : FIRST + CELLS])
        return jnp.concatenate(parts, axis=0)

    def spread_of(values):
        def of(which):
            for column in which:
                for i, rest in enumerate(values(column)):
                    for part in range(3):
                        held = rest.astype(jnp.bfloat16).astype(F32)
                        cell_parts[column, pl.ds(3 * i + part, 80, stride=PARTS), :] = held
                        rest = rest - held
                cell_parts[column, pl.ds(ONE, 80, stride=PARTS), :] = jnp.ones((80, SLOTS), F32)

        return of

    def density_shared(near, approach, at):
        support = jnp.maximum(near, 0.0)
        square = support * support
        slopes[at] = square
        return square * support, square * approach

    def density_values(column):
        x, z, vx, vz = (rows[f, column] for f in (X, Z, VX, VZ))
        return x, z, vx, vz, -(x * x + z * z), vx * x + vz * z, rows[MASS, column]

    def force_values(column):
        x, z, pressure = (rows[f, column] for f in (X, Z, P3))
        return x, z, pressure, pressure * x, pressure * z, rows[WEIGHT, column]

    def first_rows(row, shift_x, shift_z):
        weight = row(WEIGHT)
        return weight, weight * row(P0)

    def next_rows(pressure_field):
        def of(row, shift_x, shift_z):
            return (row(WEIGHT) * row(pressure_field),)

        return of

    def force_shared(pull_x, pull_z, at):
        square = slopes[at]
        return square * pull_x, square * pull_z

    send(0)
    local.wait()
    run(
        Phase(2, (), MASS, density_shared, form=0),
        0,
        spread_of(density_values),
    )
    live_mass = own_rows(MASS)
    alive = live_mass > 0.0
    density = jnp.where(alive, sums(0), 0.0)
    diverge = -6.0 * sums(1)
    ratio = density / REST_DENSITY
    for c in (0, 1):
        ratio_out[c] = ratio[c * CELLS : (c + 1) * CELLS]
    weight = jnp.where(alive, 6.0 * live_mass / jnp.where(alive, density, 1.0), 0.0)
    set_own(WEIGHT, weight)
    send(1)
    kept[0] = jnp.where(alive, (density + TIME_STEP * diverge - REST_DENSITY) / REST_DENSITY, 0.0)
    for sweep in range(ITERS):
        pressure_field = P0 if sweep == 0 else P0 + 1 + sweep
        if sweep == 0:
            phase = Phase(
                2,
                (0, 1),
                first_rows,
                lambda a, b, at: (slopes[at],) * 2,
                lambda b: b,
                lambda a: a,
            )
            moved = lambda column: (rows[WEIGHT, column], rows[WEIGHT, column] * rows[P0, column])
        else:
            phase = Phase(
                1,
                (0,),
                next_rows(pressure_field),
                lambda a, b, at: (slopes[at],),
                lambda b: b,
                lambda a: a,
            )
            moved = lambda column, f=pressure_field: (rows[WEIGHT, column] * rows[f, column],)
        run(phase, 1 + sweep, spread_of(moved))
        if sweep == 0:
            kept[1] = COMPRESSION + sums(0)
            pulled = sums(1)
        else:
            pulled = sums(0)
        updated = (1.0 - RELAXATION) * own_rows(pressure_field) + RELAXATION * (kept[0] + pulled) / kept[1]
        pressure = jnp.where(own_rows(MASS) > 0.0, updated, 0.0)
        set_own(P1 + sweep, pressure)
        send(2 + sweep)
    for c in (0, 1):
        pressure_out[c] = pressure[c * CELLS : (c + 1) * CELLS]
    run(
        Phase(2, (), WEIGHT, force_shared, form=1),
        4,
        spread_of(force_values),
    )

    live_mass = own_rows(MASS)
    alive = live_mass > 0.0
    for o in (0, 1):
        accel = jnp.where(alive, sums(o), 0.0)
        pulled = accel - GRAVITY if o == 1 else accel
        velocity_new = jnp.where(alive, own_rows(VX + o) + TIME_STEP * pulled, 0.0)
        offsets_new = jnp.where(alive, own_rows(X + o) + TIME_STEP * velocity_new, 0.0)
        for c in (0, 1):
            part = slice(c * CELLS, (c + 1) * CELLS)
            accel_out[o, c] = accel[part]
            velocity_out[o, c] = velocity_new[part]
            offsets_out[o, c] = offsets_new[part]
        slopes[o] = offsets_new.T
        slopes[2 + o] = velocity_new.T
    slopes[4] = own_rows(P3).T
    slopes[5] = live_mass.T

    chosen = leaving_slot[...]
    cell = chosen // SLOTS
    slot = chosen - cell * SLOTS
    lanes = lax.broadcasted_iota(jnp.int32, (8, SLOTS), 1)
    filled = lanes < leaving_count[...]
    upward = filled & (leaving_side[...] == 1)
    downward = filled & (leaving_side[...] == 0)
    sublanes = lax.broadcasted_iota(jnp.int32, (SLOTS, SLOTS), 0)
    cell_is, slot_is = [], []
    for b in range(8):
        cell_is.append(jnp.where(sublanes == cell[b : b + 1], 1.0, 0.0).astype(jnp.bfloat16))
    for comp in range(6):
        value = slopes[comp]
        high = value.astype(jnp.bfloat16)
        rest = value - high.astype(F32)
        middle = rest.astype(jnp.bfloat16)
        low = (rest - middle.astype(F32)).astype(jnp.bfloat16)
        picked = []
        for b in range(8):
            by_slot = sum(
                jnp.dot(part, cell_is[b], preferred_element_type=F32) for part in (low, middle, high)
            )
            one = jnp.where(sublanes == slot[b : b + 1], by_slot, 0.0)
            picked.append(jnp.sum(one, axis=0, keepdims=True))
        block = jnp.concatenate(picked, axis=0)
        block_send[0, comp] = jnp.where(downward, block, 0.0)
        block_send[1, comp] = jnp.where(upward, block, 0.0)

    def block_copy(n):
        return around[n], pltpu.make_async_remote_copy(
            src_ref=block_send.at[n],
            dst_ref=block_recv.at[1 - n],
            send_sem=send_sem.at[5, n],
            recv_sem=recv_sem.at[5, 1 - n],
            device_id=device(around[n]),
            device_id_type=MESH,
        )

    for n in (0, 1):
        shift, copy = block_copy(n)

        @pl.when(there(shift))
        def _(copy=copy):
            copy.start()

    for step in range(5):
        finish_sends(step)
    for n in (0, 1):
        shift, copy = block_copy(n)
        _, mirror = block_copy(1 - n)

        @pl.when(there(shift))
        def _(copy=copy, mirror=mirror):
            mirror.wait_recv()
            copy.wait_send()

    arrived_out[...] = block_recv[...]


def per_device(
    n_col,
    n_slab,
    offsets,
    velocity,
    particle_mass,
    pressure_start,
    counts,
    leaving_slot,
    leaving_count,
    leaving_side,
):
    alive = jnp.arange(SLOTS, dtype=jnp.int32)[None, None, :] < counts[:, :, None]
    live_mass = jnp.where(alive, particle_mass, 0.0)
    pressure = jnp.where(alive, pressure_start, 0.0)
    base = jnp.concatenate([offsets, velocity, live_mass[None], pressure[None]], 0)
    edges = jnp.stack([base[:, :, 0].reshape(12, SLOTS), base[:, :, CELLS - 1].reshape(12, SLOTS)])
    edges = jnp.pad(edges, ((0, 0), (0, 4), (0, 0)))
    vmem = pl.BlockSpec(memory_space=pltpu.VMEM)
    anywhere = pl.BlockSpec(memory_space=pl.ANY)
    cells = (2, CELLS, SLOTS)
    shape = lambda *s: jax.ShapeDtypeStruct(s, F32)
    results = pl.pallas_call(
        functools.partial(kernel, n_col=n_col, n_slab=n_slab),
        out_shape=(shape(*cells), shape(*cells), shape(2, *cells), shape(2, *cells), shape(2, *cells), shape(2, 6, 8, SLOTS)),
        in_specs=[anywhere, anywhere, vmem, vmem, vmem, vmem, vmem],
        out_specs=[vmem] * 6,
        scratch_shapes=[
            pltpu.VMEM((10, 4, 80, SLOTS), F32),
            pltpu.VMEM((TILES, SLOTS, SLOTS), F32),
            pltpu.VMEM((4, 80 * PARTS, SLOTS), F32),
            pltpu.VMEM((PARTS, FIELDS * SLOTS), jnp.bfloat16),
            pltpu.VMEM((2, SLOTS, SLOTS), F32),
            pltpu.VMEM((4, FIELDS, BLOCKS, 8, SLOTS), F32),
            pltpu.VMEM((4, SLOTS, SLOTS), jnp.bfloat16),
            pltpu.VMEM((4, 5, 2 * HALF, SLOTS), jnp.bfloat16),
            pltpu.VMEM((4, 2, BLOCKS, 8, SLOTS), F32),
            pltpu.VMEM((2, 2, SLOTS, SLOTS), F32),
            pltpu.VMEM((2, 2, CELLS + 2 * PAD, 8, SLOTS), F32),
            pltpu.VMEM((4, 2, 8, SLOTS), F32),
            pltpu.VMEM((6, 16, SLOTS), F32),
            pltpu.VMEM((4, 6, 8, SLOTS), F32),
            pltpu.VMEM((2, 6, 8, SLOTS), F32),
            pltpu.VMEM((2, 6, 8, SLOTS), F32),
            pltpu.SemaphoreType.DMA((1,)),
            pltpu.SemaphoreType.DMA((6, 8)),
            pltpu.SemaphoreType.DMA((6, 8)),
        ],
        compiler_params=pltpu.CompilerParams(
            collective_id=0, has_side_effects=True, vmem_limit_bytes=67_000_000
        ),
    )(
        base,
        edges,
        leaving_slot.reshape(8, SLOTS),
        jnp.broadcast_to(leaving_count, (8, SLOTS)),
        jnp.broadcast_to(leaving_side, (8, SLOTS)),
        *form_matrices(),
    )
    return (*results[:5], results[5].reshape(2, 6, 8, 1, SLOTS))


def solution(mesh):
    return jax.shard_map(
        functools.partial(per_device, mesh.shape["col"], mesh.shape["slab"]),
        mesh=mesh,
        in_specs=(
            P(None, "col", "slab", None),
            P(None, "col", "slab", None),
            P("col", "slab", None),
            P("col", "slab", None),
            P("col", "slab"),
            P("col", "slab", None),
            P("col", "slab"),
            P("col", "slab"),
        ),
        out_specs=(
            P("col", "slab", None),
            P("col", "slab", None),
            P(None, "col", "slab", None),
            P(None, "col", "slab", None),
            P(None, "col", "slab", None),
            P(None, None, "col", "slab", None),
        ),
        check_vma=False,
    )
```

```python
import functools

import jax
import jax.numpy as jnp
import numpy as np
from jax import lax
from jax.experimental import pallas as pl
from jax.experimental.pallas import tpu as pltpu
from jax.sharding import PartitionSpec as P

ITERS = 3
TIME_STEP = 0.1
REST_DENSITY = 50.0
COMPRESSION = 2.0
RELAXATION = 0.5
GRAVITY = 1.0

MESH = pl.DeviceIdType.MESH
F32 = jnp.float32

X, Z, VX, VZ, MASS, P0, WEIGHT, P1, P2, P3 = range(10)
FIRST = 8
CELLS = 64
SLOTS = 128
BLOCKS = 16

OWN_TILES = (
    ((1, 0, False, True), (1, 1, True, True), (2, -1, True, True), (2, 0, True, True), (2, 1, True, True)),
    ((2, 0, False, True), (2, 1, True, True)),
)
HALO_TILES = (
    ((1, 1, True, False), (1, 0, True, False), (1, -1, True, False)),
    ((2, 1, True, False), (2, 0, True, False), (2, -1, True, False)),
)
EXTRA = (
    (1, -1, ((1, 1, True, False), (2, 1, True, False))),
    (2, -1, ((2, 1, True, False),)),
    (1, CELLS, ((2, -1, True, False),)),
)
OWN0, OWN1, HALO0, HALO1 = 0, 320, 448, 646
TILES = 844
EXTRA_AT = (HALO0 + 1, HALO1 + 1, HALO1 + 2)
PAD = 2
FIELDS = 2
PARTS = 24

ONE = 21
SIX = ((0, 0), (0, 1), (1, 0), (1, 1), (0, 2), (2, 0))
FOUR = ((0, 0), (0, 1), (1, 0), (1, 1))
HALF = 32


def density_pairs(sx, sz):
    x, z, vx, vz, u, e = 0, 3, 6, 9, 12, 15
    near = [(ONE, ONE, 1 - sx * sx - sz * sz)]
    approach = []
    for a in range(3):
        near += [(u + a, ONE, 1), (ONE, u + a, 1)]
        approach += [(e + a, ONE, 1), (ONE, e + a, 1)]
    for f, v, s in ((x, vx, sx), (z, vz, sz)):
        near += [(f + a, f + b, 2) for a, b in SIX]
        approach += [(v + a, f + b, -1) for a, b in FOUR] + [(f + a, v + b, -1) for a, b in FOUR]
        for a in range(3):
            near += [(f + a, ONE, 2 * s), (ONE, f + a, -2 * s)]
        for a in range(2):
            approach += [(v + a, ONE, -s), (ONE, v + a, s)]
    return near, approach


def force_pairs(sx, sz):
    halves = []
    for f, g, s in ((0, 9, sx), (3, 12, sz)):
        half = [(f + a, 6 + b, 1) for a, b in SIX] + [(6 + a, f + b, 1) for a, b in SIX]
        for a in range(3):
            half += [(ONE, g + a, -1), (g + a, ONE, -1), (ONE, 6 + a, -s), (6 + a, ONE, s)]
        halves.append(half)
    return halves


def form_matrices():
    mine = np.zeros((2, PARTS, 2 * SLOTS), np.float32)
    others = np.zeros((2, 9, 2 * HALF, PARTS), np.float32)
    for form, (pairs, spread) in enumerate(((density_pairs, 18), (force_pairs, 15))):
        mine[form, spread : spread + 3, SLOTS:] = 1.0
        for sx in (-1, 0, 1):
            for sz in (-1, 0, 1):
                for half, terms in enumerate(pairs(sx, sz)):
                    for i, (a, b, factor) in enumerate(terms):
                        at = i + half * HALF
                        mine[form, a, at] = 1.0
                        others[form, (sx + 1) * 3 + sz + 1, at, b] = factor
    return jnp.asarray(mine, jnp.bfloat16), jnp.asarray(others, jnp.bfloat16)


class Phase:
    def __init__(self, outs, a_fields, b_rows, shared, b_factors=None, a_factors=None, form=None):
        self.outs = outs
        self.form = form
        self.a_fields = a_fields
        self.b_rows = b_rows
        self.shared = shared
        self.b_factors = b_factors
        self.a_factors = a_factors


def kernel(
    base,
    edges,
    leaving_slot,
    leaving_tags,
    mine_matrix,
    others_matrix,
    density_out,
    pressure_out,
    accel_out,
    arrived_out,
    rows,
    slopes,
    cell_parts,
    selectors,
    kept,
    lane_columns,
    lane_terms,
    tile_terms,
    lane_sums,
    column_sums,
    row_sums,
    edge_send,
    edge_recv_base,
    edge_recv,
    block_send,
    block_recv,
    local_sem,
    send_sem,
    recv_sem,
    *,
    n_col,
    n_slab,
):
    col = lax.axis_index("col")
    slab = lax.axis_index("slab")
    around = ((-1, 0), (1, 0), (0, -1), (0, 1), (-1, -1), (-1, 1), (1, -1), (1, 1))

    def there(shift):
        ok = None
        for size, me, step in ((n_col, col, shift[0]), (n_slab, slab, shift[1])):
            if step:
                one = (me > 0) if step < 0 else (me < size - 1)
                ok = one if ok is None else jnp.logical_and(ok, one)
        return ok

    def device(shift):
        return (col + shift[0], slab + shift[1])

    local = pltpu.make_async_copy(base, rows.at[X : P0 + 1, 1:3, FIRST : FIRST + CELLS, :], local_sem.at[0])
    local.start()

    zeros = jnp.zeros((8, SLOTS), F32)
    for field in range(10):
        for column in range(4):
            if column in (0, 3):

                def clear(i, carry, field=field, column=column):
                    rows[field, column, pl.ds(pl.multiple_of(i * 8, 8), 8), :] = zeros
                    return carry

                lax.fori_loop(0, 10, clear, 0)
            else:
                rows[field, column, 0:8, :] = zeros
                rows[field, column, FIRST + CELLS : FIRST + CELLS + 8, :] = zeros
    edge_recv_base[...] = jnp.zeros_like(edge_recv_base)
    edge_recv[...] = jnp.zeros_like(edge_recv)
    block_recv[...] = jnp.zeros_like(block_recv)
    for place in range(4):
        for o in (0, 1):
            lane_sums[place, o] = jnp.zeros((BLOCKS, 8, SLOTS), F32)
    for o in (0, 1):
        for c in (0, 1):
            column_sums[o, c] = jnp.zeros((SLOTS, SLOTS), F32)

    def clear_parts(i, carry):
        for column in range(4):
            cell_parts[column, pl.ds(pl.multiple_of(i * 8, 8), 8), :] = zeros
        return carry

    lax.fori_loop(0, 80 * PARTS // 8, clear_parts, 0)
    part_of = lax.broadcasted_iota(jnp.int32, (PARTS, SLOTS), 0)
    for i in range(FIELDS):
        mine = (part_of >= 3 * i) & (part_of < 3 * i + 3)
        selectors[:, i * SLOTS : (i + 1) * SLOTS] = jnp.where(mine, 1.0, 0.0).astype(jnp.bfloat16)

    barrier = pltpu.get_barrier_semaphore()
    for shift in around:

        @pl.when(there(shift))
        def _(shift=shift):
            pl.semaphore_signal(barrier, inc=1, device_id=device(shift), device_id_type=MESH)

    peers = sum(jnp.where(there(shift), 1, 0).astype(jnp.int32) for shift in around)

    def copy_of(step, n):
        shift = around[n]
        back = around.index((-shift[0], -shift[1]))
        if n < 2:
            own, far = (1, 3) if n == 0 else (2, 0)
            if step == 0:
                src = base.at[:, own - 1]
                dst = rows.at[X : P0 + 1, far, FIRST : FIRST + CELLS, :]
            else:
                src = rows.at[P0 + step, own, FIRST : FIRST + CELLS, :]
                dst = rows.at[P0 + step, far, FIRST : FIRST + CELLS, :]
        else:
            side = 0 if shift[1] < 0 else 1
            if step == 0:
                src = edges.at[side]
                dst = edge_recv_base.at[back - 2]
            else:
                src = edge_send.at[step - 1, side]
                dst = edge_recv.at[step - 1, back - 2]
        return shift, pltpu.make_async_remote_copy(
            src_ref=src,
            dst_ref=dst,
            send_sem=send_sem.at[step, n],
            recv_sem=recv_sem.at[step, back],
            device_id=device(shift),
            device_id_type=MESH,
        )

    def send(step):
        if step > 0:
            for side, at in ((0, FIRST), (1, FIRST + CELLS - 1)):
                for c in (0, 1):
                    edge_send[step - 1, side, c : c + 1, :] = rows[P0 + step, 1 + c, at : at + 1, :]
        for n in (2, 3, 0, 1, 4, 5, 6, 7):
            shift, copy = copy_of(step, n)

            @pl.when(there(shift))
            def _(copy=copy):
                copy.start()

    def receive(step, which):
        for n in which:
            shift, _ = copy_of(step, n)
            back = around.index((-shift[0], -shift[1]))
            _, mirror = copy_of(step, back)

            @pl.when(there(shift))
            def _(mirror=mirror):
                mirror.wait_recv()

        for n in which:
            if n < 2:
                continue
            shift = around[n]
            at = FIRST - 1 if shift[1] < 0 else FIRST + CELLS
            take = {0: ((1, 0), (2, 1)), -1: ((0, 1),), 1: ((3, 0),)}[shift[0]]
            for mine, theirs in take:
                if step == 0:
                    for field in range(6):
                        at_row = field * 2 + theirs
                        rows[field, mine, at : at + 1, :] = edge_recv_base[n - 2, at_row : at_row + 1, :]
                else:
                    rows[P0 + step, mine, at : at + 1, :] = edge_recv[step - 1, n - 2, theirs : theirs + 1, :]

    def finish_sends(step):
        for n in range(8):
            shift, copy = copy_of(step, n)

            @pl.when(there(shift))
            def _(copy=copy):
                copy.wait_send()

    def own_rows(field):
        return jnp.concatenate([rows[field, c, FIRST : FIRST + CELLS, :] for c in (1, 2)], axis=0)

    def set_own(field, value):
        for c in (0, 1):
            rows[field, 1 + c, FIRST : FIRST + CELLS, :] = value[c * CELLS : (c + 1) * CELLS]

    def prepare(phase, column, k, place, tiles):
        fields = len(phase.a_fields)
        at = pl.multiple_of((k + FIRST) * PARTS, PARTS)
        parts = cell_parts[column, pl.ds(at, PARTS), :].astype(jnp.bfloat16)
        if phase.form is not None:
            spread = lax.dot_general(
                parts, mine_matrix[phase.form], (((0,), (0,)), ((), ())), preferred_element_type=F32
            )
            lane_terms[place] = spread[:, :SLOTS].astype(jnp.bfloat16)
            for i, (other, dk, _, _) in enumerate(tiles):
                at = pl.multiple_of((k + (FIRST + dk)) * PARTS, PARTS)
                parts = cell_parts[other, pl.ds(at, PARTS), :].astype(jnp.bfloat16)
                matrix = others_matrix[phase.form, (other - column + 1) * 3 + dk + 1]
                tile_terms[place, i] = jnp.dot(matrix, parts, preferred_element_type=F32).astype(jnp.bfloat16)
            for b in range(BLOCKS):
                lane_columns[place, 0, b] = spread[b * 8 : b * 8 + 8, SLOTS:]
            return
        spread = lax.dot_general(parts, selectors[:, 0 : fields * SLOTS], (((0,), (0,)), ((), ())), preferred_element_type=F32)
        for i in range(fields):
            for b in range(BLOCKS):
                lane_columns[place, i, b] = spread[b * 8 : b * 8 + 8, i * SLOTS : (i + 1) * SLOTS]

    def compute_form(phase, column, k, tiles, tile0, place):
        outs = phase.outs
        terms = lane_terms[place, :, : 2 * HALF]
        blank = jnp.zeros((HALF, SLOTS), jnp.bfloat16)

        def product_of(i):
            left = jnp.concatenate([tile_terms[place, i, :HALF], blank], axis=0)
            right = jnp.concatenate([blank, tile_terms[place, i, HALF:]], axis=0)
            return jnp.dot(terms, jnp.concatenate([left, right], axis=1), preferred_element_type=F32)

        following = product_of(0)
        for i, (other, dk, give, take) in enumerate(tiles):
            product = following
            if i + 1 < len(tiles):
                following = product_of(i + 1)
            if take:
                b_factor = jnp.broadcast_to(
                    rows[phase.b_rows, other, pl.ds(k + (FIRST + dk), 1), :], (8, SLOTS)
                )
            given = [[None, None] for _ in range(outs)]
            for b in range(BLOCKS):
                block = slice(b * 8, b * 8 + 8)
                shared = phase.shared(product[block, :SLOTS], product[block, SLOTS:], (tile0 + i, block))
                for o in range(outs):
                    if take:
                        term = shared[o] * b_factor
                        lane_sums[place, o, b] = term if i == 0 else lane_sums[place, o, b] + term
                    if give:
                        term = shared[o] * lane_columns[place, 0, b]
                        so_far = given[o][b % 2]
                        given[o][b % 2] = term if so_far is None else so_far + term
            if give:
                for o in range(outs):
                    at = (o, other - 1, k + (PAD + dk))
                    row_sums[at] = row_sums[at] + (given[o][0] + given[o][1])

    def compute(phase, column, k, tiles, tile0, place):
        if phase.form is not None:
            compute_form(phase, column, k, tiles, tile0, place)
            return
        outs = phase.outs
        b_rows, theirs = [], []
        for other, dk, _, _ in tiles:

            def row(field, other=other, dk=dk):
                return jnp.broadcast_to(rows[field, other, pl.ds(k + (FIRST + dk), 1), :], (8, SLOTS))

            b_rows.append(phase.b_rows(row, float(other - column), float(dk)))
            theirs.append([[None, None] for _ in range(outs)])
        for b in range(BLOCKS):
            a = [lane_columns[place, i, b] for i in range(len(phase.a_fields))]
            a_factors = phase.a_factors(a)
            mine = [None] * outs
            for i, (_, _, give, take) in enumerate(tiles):
                shared = phase.shared(a, b_rows[i], (tile0 + i, slice(b * 8, b * 8 + 8)))
                for o in range(outs):
                    if take:
                        term = shared[o] * phase.b_factors(b_rows[i])[o]
                        mine[o] = term if mine[o] is None else mine[o] + term
                    if give:
                        term = shared[o] * a_factors[o]
                        so_far = theirs[i][o][b % 2]
                        theirs[i][o][b % 2] = term if so_far is None else so_far + term
            for o in range(outs):
                if mine[o] is not None:
                    lane_sums[place, o, b] = mine[o]
        for i, (other, dk, give, _) in enumerate(tiles):
            if give:
                for o in range(outs):
                    at = (o, other - 1, k + (PAD + dk))
                    row_sums[at] = row_sums[at] + (theirs[i][o][0] + theirs[i][o][1])

    def collect(phase, column, k, place):
        here = lax.broadcasted_iota(jnp.int32, (8, SLOTS), 1) == k + FIRST
        for b in range(BLOCKS):
            for o in range(phase.outs):
                total = jnp.sum(lane_sums[place, o, b], axis=1, keepdims=True)
                at = (o, column - 1, slice(b * 8, b * 8 + 8), slice(None))
                column_sums[at] = jnp.where(here, total, column_sums[at])

    def run(phase, step, transpose, early=None):
        def clear(i, carry):
            for o in range(phase.outs):
                row_sums[o, 0, i] = zeros
                row_sums[o, 1, i] = zeros
            return carry

        lax.fori_loop(0, CELLS + 2 * PAD, clear, 0)
        transpose((1, 2))

        def prepare_own(k, parity):
            prepare(phase, 1, k, 2 * parity, OWN_TILES[0])
            prepare(phase, 2, k, 2 * parity + 1, OWN_TILES[1])

        def compute_own(k, parity):
            compute(phase, 1, k, OWN_TILES[0], OWN0 + 5 * k, 2 * parity)
            compute(phase, 2, k, OWN_TILES[1], OWN1 + 2 * k, 2 * parity + 1)

        def collect_own(k, parity):
            collect(phase, 1, k, 2 * parity)
            collect(phase, 2, k, 2 * parity + 1)

        def own(i, carry):
            for parity in (0, 1):
                k = 1 + 2 * i + parity
                collect_own(k - 2, parity)
                compute_own(k, parity)
                prepare_own(k + 2, parity)
            return carry

        prepare_own(1, 0)
        prepare_own(2, 1)
        begin = 0
        if early is not None:
            begin = 3
            lax.fori_loop(0, begin, own, 0)
            early()
        lax.fori_loop(begin, (CELLS - 2) // 2, own, 0)
        collect_own(CELLS - 3, 0)
        collect_own(CELLS - 2, 1)

        receive(step, range(8))
        transpose((0, 1, 2, 3))

        def ends(i, carry):
            k = i * (CELLS - 1)
            prepare_own(k, 0)
            compute_own(k, 0)
            collect_own(k, 0)
            return carry

        lax.fori_loop(0, 2, ends, 0)
        def prepare_halo(k, parity):
            prepare(phase, 0, k, 2 * parity, HALO_TILES[0])
            prepare(phase, 3, k, 2 * parity + 1, HALO_TILES[1])

        def halo(i, carry):
            for parity in (0, 1):
                k = 2 * i + parity - 1
                compute(phase, 0, k, HALO_TILES[0], HALO0 + 3 * (k + 1), 2 * parity)
                compute(phase, 3, k, HALO_TILES[1], HALO1 + 3 * (k + 1), 2 * parity + 1)
                prepare_halo(k + 2, parity)
            return carry

        prepare_halo(-1, 0)
        prepare_halo(0, 1)
        lax.fori_loop(0, (CELLS + 2) // 2, halo, 0)
        for i, (column, k, tiles) in enumerate(EXTRA):
            prepare(phase, column, k, i, tiles)
        for i, (column, k, tiles) in enumerate(EXTRA):
            compute(phase, column, k, tiles, EXTRA_AT[i], i)

    def sums(o):
        parts = []
        for c in (0, 1):
            by_row = jnp.sum(row_sums[o, c, PAD : PAD + CELLS], axis=1)
            parts.append(by_row + column_sums[o, c].T[FIRST : FIRST + CELLS])
        return jnp.concatenate(parts, axis=0)

    def spread_of(values):
        def of(which):
            for column in which:
                for i, rest in enumerate(values(column)):
                    for part in range(3):
                        held = rest.astype(jnp.bfloat16).astype(F32)
                        cell_parts[column, pl.ds(3 * i + part, 80, stride=PARTS), :] = held
                        rest = rest - held
                cell_parts[column, pl.ds(ONE, 80, stride=PARTS), :] = jnp.ones((80, SLOTS), F32)

        return of

    def density_shared(near, approach, at):
        support = jnp.maximum(near, 0.0)
        square = support * support
        slopes[at] = square
        return square * support, square * approach

    def density_values(column):
        x, z, vx, vz = (rows[f, column] for f in (X, Z, VX, VZ))
        return x, z, vx, vz, -(x * x + z * z), vx * x + vz * z, rows[MASS, column]

    def force_values(column):
        x, z, pressure = (rows[f, column] for f in (X, Z, P3))
        return x, z, pressure, pressure * x, pressure * z, rows[WEIGHT, column]

    def first_rows(row, shift_x, shift_z):
        weight = row(WEIGHT)
        return weight, weight * row(P0)

    def next_rows(pressure_field):
        def of(row, shift_x, shift_z):
            return (row(WEIGHT) * row(pressure_field),)

        return of

    def force_shared(pull_x, pull_z, at):
        square = slopes[at]
        return square * pull_x, square * pull_z

    def first_send():
        pl.semaphore_wait(barrier, peers)
        send(0)

    local.wait()
    run(
        Phase(2, (), MASS, density_shared, form=0),
        0,
        spread_of(density_values),
        first_send,
    )
    live_mass = own_rows(MASS)
    alive = live_mass > 0.0
    density = jnp.where(alive, sums(0), 0.0)
    diverge = -6.0 * sums(1)
    for c in (0, 1):
        density_out[c] = density[c * CELLS : (c + 1) * CELLS]
    weight = jnp.where(alive, 6.0 * live_mass / jnp.where(alive, density, 1.0), 0.0)
    set_own(WEIGHT, weight)
    send(1)
    kept[0] = jnp.where(alive, (density + TIME_STEP * diverge - REST_DENSITY) / REST_DENSITY, 0.0)
    for sweep in range(ITERS):
        pressure_field = P0 if sweep == 0 else P0 + 1 + sweep
        if sweep == 0:
            phase = Phase(
                2,
                (0, 1),
                first_rows,
                lambda a, b, at: (slopes[at],) * 2,
                lambda b: b,
                lambda a: a,
            )
            moved = lambda column: (rows[WEIGHT, column], rows[WEIGHT, column] * rows[P0, column])
        else:
            phase = Phase(
                1,
                (0,),
                next_rows(pressure_field),
                lambda a, b, at: (slopes[at],),
                lambda b: b,
                lambda a: a,
            )
            moved = lambda column, f=pressure_field: (rows[WEIGHT, column] * rows[f, column],)
        run(phase, 1 + sweep, spread_of(moved))
        if sweep == 0:
            kept[1] = COMPRESSION + sums(0)
            pulled = sums(1)
        else:
            pulled = sums(0)
        updated = (1.0 - RELAXATION) * own_rows(pressure_field) + RELAXATION * (kept[0] + pulled) / kept[1]
        pressure = jnp.where(own_rows(MASS) > 0.0, updated, 0.0)
        set_own(P1 + sweep, pressure)
        send(2 + sweep)
    for c in (0, 1):
        pressure_out[c] = pressure[c * CELLS : (c + 1) * CELLS]
    run(
        Phase(2, (), WEIGHT, force_shared, form=1),
        4,
        spread_of(force_values),
    )

    live_mass = own_rows(MASS)
    alive = live_mass > 0.0
    for o in (0, 1):
        accel = jnp.where(alive, sums(o), 0.0)
        pulled = accel - GRAVITY if o == 1 else accel
        velocity_new = jnp.where(alive, own_rows(VX + o) + TIME_STEP * pulled, 0.0)
        offsets_new = jnp.where(alive, own_rows(X + o) + TIME_STEP * velocity_new, 0.0)
        for c in (0, 1):
            part = slice(c * CELLS, (c + 1) * CELLS)
            accel_out[o, c] = accel[part]
        slopes[o] = offsets_new.T
        slopes[2 + o] = velocity_new.T
    slopes[4] = own_rows(P3).T
    slopes[5] = live_mass.T

    chosen = leaving_slot[...]
    cell = chosen // SLOTS
    slot = chosen - cell * SLOTS
    lanes = lax.broadcasted_iota(jnp.int32, (8, SLOTS), 1)
    filled = lanes < leaving_tags[0]
    upward = filled & (leaving_tags[1] == 1)
    downward = filled & (leaving_tags[1] == 0)
    sublanes = lax.broadcasted_iota(jnp.int32, (SLOTS, SLOTS), 0)
    cell_is = []
    for b in range(0, 8, 2):
        pair = [jnp.where(sublanes == cell[i : i + 1], 1.0, 0.0).astype(jnp.bfloat16) for i in (b, b + 1)]
        cell_is.append(jnp.concatenate([jnp.concatenate(pair, axis=1)] * 3, axis=0))
    for comp in range(6):
        rest = slopes[comp]
        parts = []
        for _ in range(3):
            parts.append(rest.astype(jnp.bfloat16))
            rest = rest - parts[-1].astype(F32)
        parts = jnp.concatenate(parts, axis=1)
        picked = []
        for b in range(0, 8, 2):
            by_slot = jnp.dot(parts, cell_is[b // 2], preferred_element_type=F32)
            for i in (0, 1):
                one = jnp.where(sublanes == slot[b + i : b + i + 1], by_slot[:, i * SLOTS : (i + 1) * SLOTS], 0.0)
                picked.append(jnp.sum(one, axis=0, keepdims=True))
        block = jnp.concatenate(picked, axis=0)
        block_send[0, comp] = jnp.where(downward, block, 0.0)
        block_send[1, comp] = jnp.where(upward, block, 0.0)

    def block_copy(n):
        return around[n], pltpu.make_async_remote_copy(
            src_ref=block_send.at[n],
            dst_ref=block_recv.at[1 - n],
            send_sem=send_sem.at[5, n],
            recv_sem=recv_sem.at[5, 1 - n],
            device_id=device(around[n]),
            device_id_type=MESH,
        )

    for n in (0, 1):
        shift, copy = block_copy(n)

        @pl.when(there(shift))
        def _(copy=copy):
            copy.start()

    for step in range(5):
        finish_sends(step)
    for n in (0, 1):
        shift, copy = block_copy(n)
        _, mirror = block_copy(1 - n)

        @pl.when(there(shift))
        def _(copy=copy, mirror=mirror):
            mirror.wait_recv()
            copy.wait_send()

    arrived_out[...] = block_recv[...]


def per_device(
    n_col,
    n_slab,
    offsets,
    velocity,
    particle_mass,
    pressure_start,
    counts,
    leaving_slot,
    leaving_count,
    leaving_side,
):
    alive = jnp.arange(SLOTS, dtype=jnp.int32)[None, None, :] < counts[:, :, None]
    live_mass = jnp.where(alive, particle_mass, 0.0)
    pressure = jnp.where(alive, pressure_start, 0.0)
    base = jnp.concatenate([offsets, velocity, live_mass[None], pressure[None]], 0)
    edges = jnp.stack([base[:, :, 0].reshape(12, SLOTS), base[:, :, CELLS - 1].reshape(12, SLOTS)])
    edges = jnp.pad(edges, ((0, 0), (0, 4), (0, 0)))
    vmem = pl.BlockSpec(memory_space=pltpu.VMEM)
    anywhere = pl.BlockSpec(memory_space=pl.ANY)
    cells = (2, CELLS, SLOTS)
    shape = lambda *s: jax.ShapeDtypeStruct(s, F32)
    results = pl.pallas_call(
        functools.partial(kernel, n_col=n_col, n_slab=n_slab),
        out_shape=(shape(*cells), shape(*cells), shape(2, *cells), shape(2, 6, 8, SLOTS)),
        in_specs=[anywhere, anywhere, vmem, vmem, vmem, vmem],
        out_specs=[vmem] * 4,
        scratch_shapes=[
            pltpu.VMEM((10, 4, 80, SLOTS), F32),
            pltpu.VMEM((TILES, SLOTS, SLOTS), F32),
            pltpu.VMEM((4, 80 * PARTS, SLOTS), F32),
            pltpu.VMEM((PARTS, FIELDS * SLOTS), jnp.bfloat16),
            pltpu.VMEM((2, SLOTS, SLOTS), F32),
            pltpu.VMEM((4, FIELDS, BLOCKS, 8, SLOTS), F32),
            pltpu.VMEM((4, SLOTS, SLOTS), jnp.bfloat16),
            pltpu.VMEM((4, 5, 2 * HALF, SLOTS), jnp.bfloat16),
            pltpu.VMEM((4, 2, BLOCKS, 8, SLOTS), F32),
            pltpu.VMEM((2, 2, SLOTS, SLOTS), F32),
            pltpu.VMEM((2, 2, CELLS + 2 * PAD, 8, SLOTS), F32),
            pltpu.VMEM((4, 2, 8, SLOTS), F32),
            pltpu.VMEM((6, 16, SLOTS), F32),
            pltpu.VMEM((4, 6, 8, SLOTS), F32),
            pltpu.VMEM((2, 6, 8, SLOTS), F32),
            pltpu.VMEM((2, 6, 8, SLOTS), F32),
            pltpu.SemaphoreType.DMA((1,)),
            pltpu.SemaphoreType.DMA((6, 8)),
            pltpu.SemaphoreType.DMA((6, 8)),
        ],
        compiler_params=pltpu.CompilerParams(
            collective_id=0, has_side_effects=True, vmem_limit_bytes=67_000_000
        ),
    )(
        base,
        edges,
        leaving_slot.reshape(8, SLOTS),
        jnp.broadcast_to(jnp.stack([leaving_count, leaving_side]), (2, 8, SLOTS)),
        *form_matrices(),
    )
    density, pressure, pull, arrived = results
    pulled = pull - jnp.array([0.0, GRAVITY], F32)[:, None, None, None]
    alive = jnp.arange(SLOTS, dtype=jnp.int32)[None, None, :] < lax.optimization_barrier(counts)[:, :, None]
    velocity_new = jnp.where(alive[None], velocity + TIME_STEP * pulled, 0.0)
    offsets_new = jnp.where(alive[None], offsets + TIME_STEP * velocity_new, 0.0)
    return (
        density / REST_DENSITY,
        jnp.where(alive, pressure, 0.0),
        jnp.where(alive[None], pull, 0.0),
        velocity_new,
        offsets_new,
        arrived.reshape(2, 6, 8, 1, SLOTS),
    )


def solution(mesh):
    return jax.shard_map(
        functools.partial(per_device, mesh.shape["col"], mesh.shape["slab"]),
        mesh=mesh,
        in_specs=(
            P(None, "col", "slab", None),
            P(None, "col", "slab", None),
            P("col", "slab", None),
            P("col", "slab", None),
            P("col", "slab"),
            P("col", "slab", None),
            P("col", "slab"),
            P("col", "slab"),
        ),
        out_specs=(
            P("col", "slab", None),
            P("col", "slab", None),
            P(None, "col", "slab", None),
            P(None, "col", "slab", None),
            P(None, "col", "slab", None),
            P(None, None, "col", "slab", None),
        ),
        check_vma=False,
    )
```
